32 devices in a mesh: grid: 8 (over z, y), vec: 4 (over x, core).
Axes of the slice: x: 2, y: 2, z: 4, core: 2. Of those that a mesh axis runs over, the one named last changes fastest.
Arguments:
- trial_block: float32 [16, 48, 32, 128], P('vec', 'grid'), may hold values from -60 to 60, as said below
- response_weight: float32 [48, 32, 128], P('grid'), may hold values from 2 to 5
Outputs:
- rotated: float32 [16, 48, 32, 128], P('vec', 'grid')
- potentials: float32 [16, 48, 32, 128], P('vec', 'grid')
- ritz_matrix: float32 [16, 16], replicated
The draws below stay inside these ranges and needn't reach their ends.
Inputs may be any that keep to these rules, and one draw needn't show every extreme that they name: `trial_block`: trial vectors whose Gram matrix is positive definite.
All inputs are finite; a program needn't handle non-finite values.
Results may differ from the reference program's by a relative error of at most 0.0002.
Values sent between devices are 32-bit elements; how exact they have to be, the bound alone decides.
A program may use at most 64 MiB of HBM per device.

```python
import math
import jax
import jax.numpy as jnp
from jax import lax

NVEC = 16
ITERS = 3
BX = 6
BY = 32
NZ = 128
GY = 2
GX = 4
NX = 24
NY = 64
ROWS = 48


def draw_trial_block(key, part):
    key_list = jax.random.split(jax.random.fold_in(key, 11), 9)
    shape = (NVEC, NX, NY, NZ)
    base_noise = jnp.clip(jax.random.normal(key_list[0], shape, jnp.float32), -6.0, 6.0)
    mix_weight = 0.3
    mixing = jnp.eye(NVEC, dtype=jnp.float32) + mix_weight * jax.random.normal(key_list[1], (NVEC, NVEC), jnp.float32) / jnp.sqrt(NVEC * 1.0)
    rough = jnp.tensordot(mixing, base_noise, axes=(1, 0), precision=lax.Precision.HIGHEST)
    coord_x = (jnp.arange(NX, dtype=jnp.float32) + 0.5) / NX
    coord_y = (jnp.arange(NY, dtype=jnp.float32) + 0.5) / NY
    coord_z = (jnp.arange(NZ, dtype=jnp.float32) + 0.5) / NZ
    tilt_share = jax.random.uniform(key_list[2], (NVEC,), jnp.float32, 0.2, 0.8)
    flip_side = jax.random.randint(key_list[3], (NVEC,), 0, 2).astype(jnp.float32)
    slope = tilt_share[:, None, None] * coord_x[None, :, None] + (1.0 - tilt_share)[:, None, None] * coord_y[None, None, :]
    slope = flip_side[:, None, None] * (1.0 - slope) + (1.0 - flip_side[:, None, None]) * slope
    envelope = jnp.exp(2.3025851 * (slope - 1.0))
    waves = jax.random.randint(key_list[4], (3, NVEC, 3), 1, 4).astype(jnp.float32)
    phases = jax.random.uniform(key_list[5], (3, NVEC), jnp.float32, 0.0, 6.2831853)
    smooth_gain = jnp.exp(jax.random.uniform(key_list[6], (NVEC,), jnp.float32, -1.2039728, 0.9162907))
    smooth = jnp.zeros(shape, jnp.float32)
    for mode_index in range(3):
        wave_x = waves[mode_index, :, 0][:, None, None, None] * coord_x[None, :, None, None]
        wave_y = waves[mode_index, :, 1][:, None, None, None] * coord_y[None, None, :, None]
        wave_z = waves[mode_index, :, 2][:, None, None, None] * coord_z[None, None, None, :]
        wave_angle = 6.2831853 * (wave_x + wave_y + wave_z) + phases[mode_index][:, None, None, None]
        smooth = smooth + 0.8 * jnp.cos(wave_angle)
    scales = jnp.exp(jax.random.uniform(key_list[8], (NVEC,), jnp.float32, 0.0, 1.3862944))
    total = envelope[:, :, :, None] * rough + smooth_gain[:, None, None, None] * smooth
    result = jnp.clip(scales[:, None, None, None] * total, -60.0, 60.0)
    blocks = result.reshape(NVEC, GX, BX, GY, BY, NZ)
    stored = jnp.swapaxes(blocks, 2, 3).reshape(NVEC, GX * GY * BX, BY, NZ)
    return stored.astype(jnp.float32)


def block_scale(key, dims, cuts, least, largest):
    factor_of, own = 1.0, jax.random.fold_in(key, 6)
    for dim, shards_of in cuts:
        draws = jnp.exp(jax.random.uniform(jax.random.fold_in(own, dim), (shards_of,), jnp.float32, least / len(cuts), largest / len(cuts)))
        factor_of = factor_of * jnp.repeat(draws, dims[dim] // shards_of).reshape([-1 if axis == dim else 1 for axis in range(len(dims))])
    return factor_of


def setup_inputs(seed: int = 0) -> dict:
    arg_keys = jax.random.split(jax.random.key(seed), 3)
    trial_block = draw_trial_block(jax.random.fold_in(arg_keys[2], 71), 0)
    response_weight = jnp.clip(jnp.exp(math.log(5.0) - 0.916290732 * jax.random.uniform(arg_keys[1], (ROWS, BY, NZ), jnp.float32) ** block_scale(arg_keys[1], (ROWS, BY, NZ), ((0, 8),), -0.2, 0.2)), 2.0, 5.0)
    return {"trial_block": trial_block, "response_weight": response_weight}


COEFFS = (-5369.0 / 1800.0, 12.0 / 7.0, -15.0 / 56.0, 10.0 / 189.0, -1.0 / 112.0, 2.0 / 1925.0, -1.0 / 16632.0)

def to_grid(field):
    leading = field.shape[:-3]
    blocks = field.reshape(leading + (GX, GY, BX, BY, NZ))
    return jnp.swapaxes(blocks, -4, -3).reshape(leading + (NX, NY, NZ))

def to_store(field):
    leading = field.shape[:-3]
    blocks = field.reshape(leading + (GX, BX, GY, BY, NZ))
    return jnp.swapaxes(blocks, -4, -3).reshape(leading + (GX * GY * BX, BY, NZ))

def along_axis(total, padded, axis, length):
    for offset in range(1, 7):
        upper = lax.slice_in_dim(padded, 6 + offset, 6 + offset + length, axis=axis)
        lower = lax.slice_in_dim(padded, 6 - offset, 6 - offset + length, axis=axis)
        total = total + COEFFS[offset] * (upper + lower)
    return total

def operate(field):
    total = 3.0 * COEFFS[0] * field
    padded_x = jnp.concatenate([field[NX - 6:], field, field[:6]], axis=0)
    total = along_axis(total, padded_x, 0, NX)
    sheared_up = jnp.roll(field, -BX, axis=0)
    sheared_down = jnp.roll(field, BX, axis=0)
    padded_y = jnp.concatenate([sheared_down[:, NY - 6:], field, sheared_up[:, :6]], axis=1)
    total = along_axis(total, padded_y, 1, NY)
    padded_z = jnp.pad(field, ((0, 0), (0, 0), (6, 6)))
    total = along_axis(total, padded_z, 2, NZ)
    return -total

def solve_one(source):
    solution = jnp.zeros_like(source)
    residual = source
    direction = source
    norm_now = jnp.sum(residual * residual)
    for step in range(ITERS):
        image = operate(direction)
        alpha = norm_now / jnp.sum(direction * image)
        solution = solution + alpha * direction
        residual = residual - alpha * image
        norm_next = jnp.sum(residual * residual)
        direction = residual + norm_next / norm_now * direction
        norm_now = norm_next
    return solution

def reference(trial_block, response_weight):
    weight_grid = to_grid(response_weight)
    phi_grid = lax.map(lambda vector: solve_one(weight_grid * vector), to_grid(trial_block))
    phi = to_store(phi_grid)
    cells = NX * NY * NZ
    flat_x = trial_block.reshape(NVEC, -1)
    flat_p = phi.reshape(NVEC, -1)
    high = lax.Precision.HIGHEST
    gram = jnp.dot(flat_x, flat_x.T, precision=high) / cells
    cross = jnp.dot(flat_x, flat_p.T, precision=high) / cells
    lower = jnp.linalg.cholesky(gram)
    inverse = lax.linalg.triangular_solve(lower, jnp.eye(NVEC, dtype=jnp.float32), left_side=True, lower=True)
    middle = jnp.dot(inverse, 0.5 * (cross + cross.T), precision=high)
    ritz_matrix = jnp.dot(middle, inverse.T, precision=high)
    rotated = jnp.dot(inverse, flat_x, precision=high).reshape(trial_block.shape)
    potentials = jnp.dot(inverse, flat_p, precision=high).reshape(trial_block.shape)
    return (rotated, potentials, ritz_matrix)
```

```python
import functools

import jax
import jax.numpy as jnp
from jax import lax
from jax.experimental import pallas as pl
from jax.experimental.pallas import tpu as pltpu
from jax.sharding import PartitionSpec as P

ITERS = 3


COEFFS = (
    -5369.0 / 1800.0,
    12.0 / 7.0,
    -15.0 / 56.0,
    10.0 / 189.0,
    -1.0 / 112.0,
    2.0 / 1925.0,
    -1.0 / 16632.0,
)


def shifted(value, axis, steps):
    count = lax.axis_size(axis)
    pairs = [(source, (source + steps) % count) for source in range(count)]
    return lax.ppermute(value, axis, pairs)


def with_halo(cells, sides, width):
    for axis, dim in sides:
        count = lax.axis_size(axis)
        head = lax.slice_in_dim(cells, 0, width, axis=dim)
        tail = lax.slice_in_dim(cells, cells.shape[dim] - width, cells.shape[dim], axis=dim)
        cells = jnp.concatenate(
            [
                lax.ppermute(tail, axis, [(i, (i + 1) % count) for i in range(count)]),
                cells,
                lax.ppermute(head, axis, [((i + 1) % count, i) for i in range(count)]),
            ],
            axis=dim,
        )
    return cells


def along_axis(total, padded, axis, length):
    for offset in range(1, 7):
        upper = lax.slice_in_dim(padded, 6 + offset, 6 + offset + length, axis=axis)
        lower = lax.slice_in_dim(padded, 6 - offset, 6 - offset + length, axis=axis)
        total = total + COEFFS[offset] * (upper + lower)
    return total


def operate(field):
    stride = max(lax.axis_size("grid") // 16, 2)
    row_count = field.shape[1]
    col_count = field.shape[2]
    total = 3.0 * COEFFS[0] * field
    below = shifted(field, "grid", stride)
    above = shifted(field, "grid", -stride)
    along_x = jnp.concatenate([below, field, above], axis=1)
    total = along_axis(total, along_x, 1, row_count)
    side_halo = with_halo(field, (("grid", 2),), 6)
    total = along_axis(total, side_halo, 2, col_count)
    along_z = jnp.pad(field, ((0, 0), (0, 0), (0, 0), (6, 6)))
    total = along_axis(total, along_z, 3, field.shape[3])
    return -total


def inner(left, right):
    return jnp.sum(left * right, axis=(1, 2, 3))


def expand(values):
    return values[:, None, None, None]


def two_products(residual, image):
    return lax.psum((inner(residual, residual), inner(residual, image)), "grid")


def finish(gram, cross, cells):
    high = lax.Precision.HIGHEST
    gram = gram / cells
    cross = cross / cells
    lower = jnp.linalg.cholesky(gram)
    inverse = lax.linalg.triangular_solve(
        lower, jnp.eye(gram.shape[0], dtype=jnp.float32), left_side=True, lower=True
    )
    middle = jnp.dot(inverse, 0.5 * (cross + cross.T), precision=high)
    return (inverse, jnp.dot(middle, inverse.T, precision=high))


def body(trial_block, response_weight):
    high = lax.Precision.HIGHEST
    source = response_weight[None] * trial_block
    solution = jnp.zeros_like(source)
    residual = source
    image = operate(residual)
    norm_now, product = two_products(residual, image)
    alpha = norm_now / product
    direction, along = (residual, image)
    for step in range(ITERS):
        solution = solution + expand(alpha) * direction
        residual = residual - expand(alpha) * along
        if step + 1 < ITERS:
            image = operate(residual)
            norm_next, product = two_products(residual, image)
            ratio = norm_next / norm_now
            alpha = norm_next / (product - ratio * norm_next / alpha)
            direction = residual + expand(ratio) * direction
            along = image + expand(ratio) * along
            norm_now = norm_next
    local_count = trial_block.shape[0]
    whole_x, whole_p = (
        lax.all_gather(trial_block, "vec", axis=0, tiled=True),
        lax.all_gather(solution, "vec", axis=0, tiled=True),
    )
    flat_x = whole_x.reshape(whole_x.shape[0], -1)
    flat_p = whole_p.reshape(whole_p.shape[0], -1)
    gram, cross = lax.psum(
        (jnp.dot(flat_x, flat_x.T, precision=high), jnp.dot(flat_x, flat_p.T, precision=high)),
        "grid",
    )
    cells = lax.axis_size("grid") * flat_x.shape[1]
    inverse, ritz_matrix = finish(gram, cross, cells)
    own_rows = lax.dynamic_slice_in_dim(
        inverse, lax.axis_index("vec") * local_count, local_count, 0
    )
    rotated = jnp.dot(own_rows, flat_x, precision=high).reshape(trial_block.shape)
    potentials = jnp.dot(own_rows, flat_p, precision=high).reshape(trial_block.shape)
    return (rotated, potentials, ritz_matrix)


MESH_ID = pl.DeviceIdType.MESH
PAD = 8
HALO = 6


def kernel(
    groups, parts, trial, weight, rotated, potentials, ritz,
    src, pad, img, dirn, along, phi, sums, sums_in, held, waves, gmsg, gin, cmsg, cin, mats, coef,
    fsend, frecv, hsend, hrecv, ssend, srecv, tsend, trecv, rsend, rrecv,
    bsend, brecv, psend, precv, xsend, xrecv, ysend, yrecv, gsend, grecv, csend, crecv,
):
    nl, rows, cols, depth = trial.shape
    nvec = parts * nl
    length = pad.shape[0]
    blocks = length // rows
    pairs = parts // 2
    total_devices = groups * parts
    me_g = lax.axis_index("grid")
    me_v = lax.axis_index("vec")
    me = me_g * parts + me_v
    pair = lax.div(me_v, 2)
    core = lax.rem(me_v, 2)
    partner = (me_g, pair * 2 + 1 - core)
    blk = lax.div(me_g, 2)
    half = lax.rem(me_g, 2)
    center = slice(PAD, PAD + cols)

    barrier = pltpu.get_barrier_semaphore()

    def device_at(k):
        target = lax.rem(me + k, total_devices)
        return (lax.div(target, parts), lax.rem(target, parts))

    def greet(k, carry):
        pl.semaphore_signal(barrier, inc=1, device_id=device_at(k), device_id_type=MESH_ID)
        return carry

    lax.fori_loop(1, total_devices, greet, 0)

    def prepare(i, carry):
        scale = weight[i]
        for s in range(nl):
            value = trial[s, i]
            src[s, i] = scale * value
            held[me_v * nl + s, i] = value
        return carry

    lax.fori_loop(0, rows, prepare, 0)
    pl.semaphore_wait(barrier, total_devices - 1)

    def remote(source, target, send, recv, device):
        return pltpu.make_async_remote_copy(
            src_ref=source, dst_ref=target, send_sem=send, recv_sem=recv,
            device_id=device, device_id_type=MESH_ID,
        )

    def forward(s):
        return remote(
            src.at[s], pad.at[pl.ds(blk * rows, rows), center], fsend.at[s], frecv.at[blk],
            (core * nl + s, pair * 2 + half),
        )

    def own_slot(s):
        return jnp.logical_and(core * nl + s == me_g, half == core)

    for step in range(nl):
        s = lax.rem(me_g + step, nl)

        @pl.when(jnp.logical_not(own_slot(s)))
        def _():
            forward(s).start()

        @pl.when(own_slot(s))
        def _():
            pad[pl.ds(blk * rows, rows), center] = src[s]

    def slot_ref(buffer, v):
        return buffer.at[pl.ds(v * nl, nl)]

    def trial_copy(q):
        device = partner if q == 0 else (me_g, lax.rem(pair + q, pairs) * 2 + core)
        return remote(trial, slot_ref(held, me_v), tsend.at[q], trecv.at[q], device)

    def from_pair(q):
        return lax.rem(pair - q + pairs, pairs) * 2 + core

    def trial_relay(q):
        v = from_pair(q)
        return remote(slot_ref(held, v), slot_ref(held, v), rsend.at[q], rrecv.at[q], partner)

    for q in list(range(1, pairs)) + [0]:
        trial_copy(q).start()

    owner_v = pair * 2 + lax.div(me_g, nl)
    for bx in range(blocks):
        @pl.when(jnp.logical_not(jnp.logical_and(bx * 2 + core == me_g, owner_v == me_v)))
        def _():
            remote(
                src.at[0], pad.at[pl.ds(bx * rows, rows), center], fsend.at[0], frecv.at[bx], partner
            ).wait_recv()

    lane = lax.broadcasted_iota(jnp.int32, (cols, depth), 1)

    def halo(side, bx):
        if side == 0:
            shift, here, there = core, slice(cols, PAD + cols), slice(0, PAD)
        else:
            shift, here, there = core - 1, slice(PAD, 2 * PAD), slice(PAD + cols, 2 * PAD + cols)
        target = lax.rem(bx + shift + blocks, blocks)
        return remote(
            pad.at[pl.ds(bx * rows, rows), here], pad.at[pl.ds(target * rows, rows), there],
            hsend.at[side, bx], hrecv.at[side, bx], partner,
        )

    halos = [(side, bx) for bx in range(blocks) for side in range(2)]

    def pass_xz(x, carry):
        value = pad[x, center]
        acc = (3.0 * COEFFS[0]) * value
        for k in range(1, HALO + 1):
            near = pad[lax.rem(x + k, length), center] + pad[lax.rem(x + length - k, length), center]
            up = jnp.where(lane < depth - k, pltpu.roll(value, depth - k, 1), 0.0)
            low = jnp.where(lane >= k, pltpu.roll(value, k, 1), 0.0)
            acc = acc + COEFFS[k] * (near + (up + low))
        img[x] = acc
        return carry

    def pass_y(x, carry):
        norm, product = carry
        acc = img[x]
        for k in range(1, HALO + 1):
            acc = acc + COEFFS[k] * (
                pad[x, PAD + k : PAD + k + cols] + pad[x, PAD - k : PAD - k + cols]
            )
        acc = -acc
        img[x] = acc
        value = pad[x, center]
        return (norm + value * value, product + value * acc)

    def folded(value):
        return value.reshape(cols // 8, 8, depth).sum(axis=0)

    def back(bx):
        return remote(
            phi.at[pl.ds(bx * rows, rows)], waves.at[pair * 2 * nl + me_g],
            bsend.at[bx], brecv.at[lax.rem(me_g, nl)], (bx * 2 + core, owner_v),
        )

    norm_now = alpha = None
    for step in range(ITERS):
        for side, bx in halos:
            halo(side, bx).start()
        lax.fori_loop(0, length, pass_xz, 0, unroll=2)
        for side, bx in halos:
            halo(side, bx).wait_recv()
        zero = jnp.zeros((cols, depth), jnp.float32)
        norm, product = lax.fori_loop(0, length, pass_y, (zero, zero), unroll=2)
        sums[step, 0] = folded(norm)
        sums[step, 1] = folded(product)
        exchange = remote(sums.at[step], sums_in.at[step], ssend.at[step], srecv.at[step], partner)
        exchange.start()
        for side, bx in halos:
            halo(side, bx).wait_send()
        if step == 0:
            for q in range(1, pairs):
                trial_copy(q).wait_recv()
                trial_relay(q).start()
        exchange.wait()
        norm_next = jnp.sum(sums[step, 0] + sums_in[step, 0], axis=(0, 1), keepdims=True)
        product = jnp.sum(sums[step, 1] + sums_in[step, 1], axis=(0, 1), keepdims=True)
        last = step + 1 == ITERS
        if step == 0:
            alpha = norm_next / product
            ratio = None
        else:
            ratio = norm_next / norm_now
            alpha = norm_next / (product - ratio * norm_next / alpha)
            ratio_wide = jnp.broadcast_to(ratio, (cols, depth))
        norm_now = norm_next
        alpha_wide = jnp.broadcast_to(alpha, (cols, depth))

        def update(x, carry):
            value = pad[x, center]
            image = img[x]
            if step == 0:
                phi[x] = alpha_wide * value
                dirn[x] = value
                along[x] = image
            else:
                value_dir = value + ratio_wide * dirn[x]
                phi[x] = phi[x] + alpha_wide * value_dir
                if not last:
                    dirn[x] = value_dir
                    image = image + ratio_wide * along[x]
                    along[x] = image
            if not last:
                pad[x, center] = value - alpha_wide * image
            return carry

        if not last:
            lax.fori_loop(0, length, update, 0, unroll=2)
        else:
            for bx in range(blocks):
                lax.fori_loop(bx * rows, (bx + 1) * rows, update, 0, unroll=2)
                own = jnp.logical_and(bx * 2 + core == me_g, owner_v == me_v)

                @pl.when(jnp.logical_not(own))
                def _():
                    back(bx).start()

                @pl.when(own)
                def _():
                    waves[pair * 2 * nl + me_g] = phi[bx * rows : (bx + 1) * rows]

    lane_row = lax.broadcasted_iota(jnp.int32, (nl, depth), 1)

    def products(buffer):
        def one(j, acc):
            other = held[j]
            parts_of = [
                jnp.sum(jnp.sum(buffer[me_v * nl + s] * other, axis=0), axis=0, keepdims=True)
                for s in range(nl)
            ]
            value = jnp.sum(jnp.concatenate(parts_of, axis=0), axis=1, keepdims=True)
            return jnp.where(lane_row == j, value, acc)

        return lax.fori_loop(0, nvec, one, jnp.zeros((nl, depth), jnp.float32), unroll=4)

    def spread(message, inbox, send, recv):
        inbox[me_g, me_v] = message[...]

        def start(k, carry):
            remote(message, inbox.at[me_g, me_v], send.at[k], recv.at[me], device_at(k)).start()
            return carry

        lax.fori_loop(1, total_devices, start, 0)

    def collect(message, inbox, send, recv, slot):
        def wait(k, carry):
            g, v = device_at(k)
            copy = remote(message, inbox.at[g, v], send.at[k], recv.at[g * parts + v], (g, v))
            copy.wait_recv()
            copy.wait_send()
            return carry

        lax.fori_loop(1, total_devices, wait, 0)
        for v in range(parts):
            total = inbox[0, v]
            for g in range(1, groups):
                total = total + inbox[g, v]
            mats[slot, v * nl : (v + 1) * nl] = total / (groups * rows * cols * depth)

    trial_copy(0).wait_recv()
    for q in range(1, pairs):
        trial_relay(q).wait_recv()
    gmsg[...] = products(held)
    spread(gmsg, gin, gsend, grecv)

    def wave_core(s):
        slot = waves.at[me_v * nl + s]
        return remote(slot, slot, psend.at[s], precv.at[s], partner)

    def wave_over(q, s):
        slot = waves.at[me_v * nl + s]
        return remote(
            slot, slot, xsend.at[q, s], xrecv.at[q, s], (me_g, lax.rem(pair + q, pairs) * 2 + core)
        )

    def wave_from(q, s):
        slot = waves.at[from_pair(q) * nl + s]
        return remote(slot, slot, xsend.at[q, s], xrecv.at[q, s], partner)

    def wave_relay(q, s):
        slot = waves.at[from_pair(q) * nl + s]
        return remote(slot, slot, ysend.at[q, s], yrecv.at[q, s], partner)

    for s in range(nl):
        @pl.when(jnp.logical_not(own_slot(s)))
        def _():
            slot = waves.at[me_v * nl + s]
            remote(phi.at[0:rows], slot, bsend.at[0], brecv.at[s], partner).wait_recv()

        for q in range(1, pairs):
            wave_over(q, s).start()
        wave_core(s).start()

    cmsg[...] = products(waves)
    spread(cmsg, cin, csend, crecv)
    for q in range(1, pairs):
        for s in range(nl):
            wave_from(q, s).wait_recv()
            wave_relay(q, s).start()

    collect(gmsg, gin, gsend, grecv, 0)
    gram = mats[0]
    row_of = lax.broadcasted_iota(jnp.int32, (nvec, depth), 0)
    lane_of = lax.broadcasted_iota(jnp.int32, (nvec, depth), 1)
    inverse = jnp.where(row_of == lane_of, 1.0, 0.0)
    for k in range(nvec):
        scale = 1.0 / jnp.sqrt(gram[k : k + 1, k : k + 1])
        column = gram[:, k : k + 1] * scale
        line = inverse[k : k + 1] * scale
        inverse = jnp.where(row_of > k, inverse - column * line, jnp.where(row_of == k, line, inverse))
        gram = gram - column * (gram[k : k + 1] * scale)
    mats[1] = inverse
    own_rows = mats[1, pl.ds(me_v * nl, nl)]
    for i in range(nvec):
        coef[i] = jnp.broadcast_to(own_rows[:, i : i + 1], (nl, depth))

    def rotate(buffer, out):
        def one(row, carry):
            totals = [None] * nl
            for i in range(nvec):
                value = buffer[i, row]
                for s in range(nl):
                    term = coef[i, s : s + 1] * value
                    totals[s] = term if i == 0 else totals[s] + term
            for s in range(nl):
                out[s, row] = totals[s]
            return carry

        lax.fori_loop(0, rows, one, 0)

    rotate(held, rotated)
    for s in range(nl):
        slot = waves.at[(pair * 2 + 1 - core) * nl + s]
        remote(slot, slot, psend.at[s], precv.at[s], partner).wait_recv()
    for q in range(1, pairs):
        for s in range(nl):
            wave_relay(q, s).wait_recv()
    rotate(waves, potentials)

    collect(cmsg, cin, csend, crecv, 2)
    cross = mats[2]
    high = lax.Precision.HIGHEST
    last_dims = (((1,), (1,)), ((), ()))
    inverse = mats[1]
    small = inverse[:, :nvec]
    middle = 0.5 * (
        jnp.dot(small, cross, precision=high)[:, :nvec]
        + lax.dot_general(inverse, cross, last_dims, precision=high)
    )
    ritz[...] = lax.dot_general(middle, small, last_dims, precision=high)

    for s in range(nl):
        @pl.when(jnp.logical_not(own_slot(s)))
        def _():
            forward(s).wait_send()

        wave_core(s).wait_send()
    for bx in range(blocks):
        @pl.when(jnp.logical_not(jnp.logical_and(bx * 2 + core == me_g, owner_v == me_v)))
        def _():
            back(bx).wait_send()
    for q in range(pairs):
        trial_copy(q).wait_send()
    for q in range(1, pairs):
        trial_relay(q).wait_send()
        for s in range(nl):
            wave_over(q, s).wait_send()
            wave_relay(q, s).wait_send()


def paired_body(trial_block, response_weight):
    nl, rows, cols, depth = trial_block.shape
    groups, parts = lax.axis_size("grid"), lax.axis_size("vec")
    nvec, blocks = parts * nl, groups // 2
    pairs, length, devices = parts // 2, (groups // 2) * rows, groups * parts
    f32 = jnp.float32
    dma = pltpu.SemaphoreType.DMA
    vmem = pl.BlockSpec(memory_space=pltpu.VMEM)
    field = pltpu.VMEM((length, cols, depth), f32)
    whole = pltpu.VMEM((nvec, rows, cols, depth), f32)
    inbox = pltpu.VMEM((groups, parts, nl, depth), f32)
    message = pltpu.VMEM((nl, depth), f32)
    small = pltpu.VMEM((ITERS, 2, 8, depth), f32)
    return pl.pallas_call(
        functools.partial(kernel, groups, parts),
        out_shape=(
            jax.ShapeDtypeStruct(trial_block.shape, f32),
            jax.ShapeDtypeStruct(trial_block.shape, f32),
            jax.ShapeDtypeStruct((nvec, nvec), f32),
        ),
        in_specs=[vmem, vmem],
        out_specs=(vmem, vmem, vmem),
        scratch_shapes=[
            pltpu.VMEM((nl, rows, cols, depth), f32),
            pltpu.VMEM((length, cols + 2 * PAD, depth), f32),
            field, field, field, field, small, small, whole, whole,
            message, inbox, message, inbox,
            pltpu.VMEM((3, nvec, depth), f32), pltpu.VMEM((nvec, nl, depth), f32),
            dma((nl,)), dma((blocks,)), dma((2, blocks)), dma((2, blocks)),
            dma((ITERS,)), dma((ITERS,)), dma((pairs,)), dma((pairs,)), dma((pairs,)), dma((pairs,)),
            dma((blocks,)), dma((nl,)), dma((nl,)), dma((nl,)),
            dma((pairs, nl)), dma((pairs, nl)), dma((pairs, nl)), dma((pairs, nl)),
            dma((devices,)), dma((devices,)), dma((devices,)), dma((devices,)),
        ],
        compiler_params=pltpu.CompilerParams(collective_id=0, has_side_effects=True),
    )(trial_block, response_weight)


def chosen_body(trial_block, response_weight):
    nl, rows, cols, depth = trial_block.shape
    groups, parts = lax.axis_size("grid"), lax.axis_size("vec")
    fits = (
        max(groups // 16, 2) == 2 and groups == 2 * nl and parts % 2 == 0 and rows == HALO
        and cols % 8 == 0 and cols >= PAD and parts * nl <= depth
    )
    return (paired_body if fits else body)(trial_block, response_weight)


def solution(mesh):
    placed = (P("vec", "grid", None, None), P("grid", None, None))
    return jax.shard_map(
        chosen_body,
        mesh=mesh,
        in_specs=placed,
        out_specs=(P("vec", "grid", None, None), P("vec", "grid", None, None), P()),
        check_vma=False,
    )
```

```python
import functools

import jax
import jax.numpy as jnp
from jax import lax
from jax.experimental import pallas as pl
from jax.experimental.pallas import tpu as pltpu
from jax.sharding import PartitionSpec as P

ITERS = 3


COEFFS = (
    -5369.0 / 1800.0,
    12.0 / 7.0,
    -15.0 / 56.0,
    10.0 / 189.0,
    -1.0 / 112.0,
    2.0 / 1925.0,
    -1.0 / 16632.0,
)


def shifted(value, axis, steps):
    count = lax.axis_size(axis)
    pairs = [(source, (source + steps) % count) for source in range(count)]
    return lax.ppermute(value, axis, pairs)


def with_halo(cells, sides, width):
    for axis, dim in sides:
        count = lax.axis_size(axis)
        head = lax.slice_in_dim(cells, 0, width, axis=dim)
        tail = lax.slice_in_dim(cells, cells.shape[dim] - width, cells.shape[dim], axis=dim)
        cells = jnp.concatenate(
            [
                lax.ppermute(tail, axis, [(i, (i + 1) % count) for i in range(count)]),
                cells,
                lax.ppermute(head, axis, [((i + 1) % count, i) for i in range(count)]),
            ],
            axis=dim,
        )
    return cells


def along_axis(total, padded, axis, length):
    for offset in range(1, 7):
        upper = lax.slice_in_dim(padded, 6 + offset, 6 + offset + length, axis=axis)
        lower = lax.slice_in_dim(padded, 6 - offset, 6 - offset + length, axis=axis)
        total = total + COEFFS[offset] * (upper + lower)
    return total


def operate(field):
    stride = max(lax.axis_size("grid") // 16, 2)
    row_count = field.shape[1]
    col_count = field.shape[2]
    total = 3.0 * COEFFS[0] * field
    below = shifted(field, "grid", stride)
    above = shifted(field, "grid", -stride)
    along_x = jnp.concatenate([below, field, above], axis=1)
    total = along_axis(total, along_x, 1, row_count)
    side_halo = with_halo(field, (("grid", 2),), 6)
    total = along_axis(total, side_halo, 2, col_count)
    along_z = jnp.pad(field, ((0, 0), (0, 0), (0, 0), (6, 6)))
    total = along_axis(total, along_z, 3, field.shape[3])
    return -total


def inner(left, right):
    return jnp.sum(left * right, axis=(1, 2, 3))


def expand(values):
    return values[:, None, None, None]


def two_products(residual, image):
    return lax.psum((inner(residual, residual), inner(residual, image)), "grid")


def finish(gram, cross, cells):
    high = lax.Precision.HIGHEST
    gram = gram / cells
    cross = cross / cells
    lower = jnp.linalg.cholesky(gram)
    inverse = lax.linalg.triangular_solve(
        lower, jnp.eye(gram.shape[0], dtype=jnp.float32), left_side=True, lower=True
    )
    middle = jnp.dot(inverse, 0.5 * (cross + cross.T), precision=high)
    return (inverse, jnp.dot(middle, inverse.T, precision=high))


def body(trial_block, response_weight):
    high = lax.Precision.HIGHEST
    source = response_weight[None] * trial_block
    solution = jnp.zeros_like(source)
    residual = source
    image = operate(residual)
    norm_now, product = two_products(residual, image)
    alpha = norm_now / product
    direction, along = (residual, image)
    for step in range(ITERS):
        solution = solution + expand(alpha) * direction
        residual = residual - expand(alpha) * along
        if step + 1 < ITERS:
            image = operate(residual)
            norm_next, product = two_products(residual, image)
            ratio = norm_next / norm_now
            alpha = norm_next / (product - ratio * norm_next / alpha)
            direction = residual + expand(ratio) * direction
            along = image + expand(ratio) * along
            norm_now = norm_next
    local_count = trial_block.shape[0]
    whole_x, whole_p = (
        lax.all_gather(trial_block, "vec", axis=0, tiled=True),
        lax.all_gather(solution, "vec", axis=0, tiled=True),
    )
    flat_x = whole_x.reshape(whole_x.shape[0], -1)
    flat_p = whole_p.reshape(whole_p.shape[0], -1)
    gram, cross = lax.psum(
        (jnp.dot(flat_x, flat_x.T, precision=high), jnp.dot(flat_x, flat_p.T, precision=high)),
        "grid",
    )
    cells = lax.axis_size("grid") * flat_x.shape[1]
    inverse, ritz_matrix = finish(gram, cross, cells)
    own_rows = lax.dynamic_slice_in_dim(
        inverse, lax.axis_index("vec") * local_count, local_count, 0
    )
    rotated = jnp.dot(own_rows, flat_x, precision=high).reshape(trial_block.shape)
    potentials = jnp.dot(own_rows, flat_p, precision=high).reshape(trial_block.shape)
    return (rotated, potentials, ritz_matrix)


MESH_ID = pl.DeviceIdType.MESH
PAD = 8
HALO = 6


def kernel(
    groups, parts, trial, weight, rotated, potentials, ritz,
    wbuf, src, pad, img, dirn, along, phi, sums, sums_in, held, waves, gmsg, gin, cmsg, cin, mats, coef,
    fsend, frecv, hsend, hrecv, ssend, srecv, tsend, trecv, rsend, rrecv,
    bsend, brecv, psend, precv, xsend, xrecv, ysend, yrecv, gsend, grecv, csend, crecv, isend,
):
    nl, rows, cols, depth = trial.shape
    nvec = parts * nl
    length = pad.shape[0]
    blocks = length // rows
    pairs = parts // 2
    total_devices = groups * parts
    me_g = lax.axis_index("grid")
    me_v = lax.axis_index("vec")
    me = me_g * parts + me_v
    pair = lax.div(me_v, 2)
    core = lax.rem(me_v, 2)
    partner = (me_g, pair * 2 + 1 - core)
    blk = lax.div(me_g, 2)
    half = lax.rem(me_g, 2)
    center = slice(PAD, PAD + cols)

    barrier = pltpu.get_barrier_semaphore()

    def device_at(k):
        target = lax.rem(me + k, total_devices)
        return (lax.div(target, parts), lax.rem(target, parts))

    def greet(k, carry):
        pl.semaphore_signal(barrier, inc=1, device_id=device_at(k), device_id_type=MESH_ID)
        return carry

    lax.fori_loop(1, total_devices, greet, 0)

    fetches = [
        pltpu.make_async_copy(weight, wbuf, isend.at[0]),
        pltpu.make_async_copy(trial, held.at[pl.ds(me_v * nl, nl)], isend.at[1]),
    ]
    for fetch in fetches:
        fetch.start()
    for fetch in fetches:
        fetch.wait()

    def prepare(i, carry):
        scale = wbuf[i]
        for s in range(nl):
            src[s, i] = scale * held[me_v * nl + s, i]
        return carry

    lax.fori_loop(0, rows, prepare, 0)
    pl.semaphore_wait(barrier, total_devices - 1)

    def remote(source, target, send, recv, device):
        return pltpu.make_async_remote_copy(
            src_ref=source, dst_ref=target, send_sem=send, recv_sem=recv,
            device_id=device, device_id_type=MESH_ID,
        )

    def forward(s):
        return remote(
            src.at[s], pad.at[pl.ds(blk * rows, rows), center], fsend.at[s], frecv.at[blk],
            (core * nl + s, pair * 2 + half),
        )

    def own_slot(s):
        return jnp.logical_and(core * nl + s == me_g, half == core)

    for step in range(nl):
        s = lax.rem(me_g + step, nl)

        @pl.when(jnp.logical_not(own_slot(s)))
        def _():
            forward(s).start()

        @pl.when(own_slot(s))
        def _():
            pad[pl.ds(blk * rows, rows), center] = src[s]

    def slot_ref(buffer, v):
        return buffer.at[pl.ds(v * nl, nl)]

    def trial_copy(q):
        device = partner if q == 0 else (me_g, lax.rem(pair + q, pairs) * 2 + core)
        return remote(slot_ref(held, me_v), slot_ref(held, me_v), tsend.at[q], trecv.at[q], device)

    def from_pair(q):
        return lax.rem(pair - q + pairs, pairs) * 2 + core

    def trial_relay(q):
        v = from_pair(q)
        return remote(slot_ref(held, v), slot_ref(held, v), rsend.at[q], rrecv.at[q], partner)

    for q in list(range(1, pairs)) + [0]:
        trial_copy(q).start()

    def halo(side, bx):
        if side == 0:
            shift, here, there = core, slice(cols, PAD + cols), slice(0, PAD)
        else:
            shift, here, there = core - 1, slice(PAD, 2 * PAD), slice(PAD + cols, 2 * PAD + cols)
        target = lax.rem(bx + shift + blocks, blocks)
        return remote(
            pad.at[pl.ds(bx * rows, rows), here], pad.at[pl.ds(target * rows, rows), there],
            hsend.at[side, bx], hrecv.at[side, bx], partner,
        )

    owner_v = pair * 2 + lax.div(me_g, nl)
    for bx in range(blocks):
        @pl.when(jnp.logical_not(jnp.logical_and(bx * 2 + core == me_g, owner_v == me_v)))
        def _():
            remote(
                src.at[0], pad.at[pl.ds(bx * rows, rows), center], fsend.at[0], frecv.at[bx], partner
            ).wait_recv()

        for side in range(2):
            halo(side, bx).start()

    lane = lax.broadcasted_iota(jnp.int32, (cols, depth), 1)

    halos = [(side, bx) for bx in range(blocks) for side in range(2)]

    def pass_xz(x, carry):
        value = pad[x, center]
        acc = (3.0 * COEFFS[0]) * value
        for k in range(1, HALO + 1):
            near = pad[lax.rem(x + k, length), center] + pad[lax.rem(x + length - k, length), center]
            up = jnp.where(lane < depth - k, pltpu.roll(value, depth - k, 1), 0.0)
            low = jnp.where(lane >= k, pltpu.roll(value, k, 1), 0.0)
            acc = acc + COEFFS[k] * (near + (up + low))
        img[x] = acc
        return carry

    def pass_y(x, carry):
        norm, product = carry
        acc = img[x]
        for k in range(1, HALO + 1):
            acc = acc + COEFFS[k] * (
                pad[x, PAD + k : PAD + k + cols] + pad[x, PAD - k : PAD - k + cols]
            )
        acc = -acc
        img[x] = acc
        value = pad[x, center]
        return (norm + value * value, product + value * acc)

    def folded(value):
        return value.reshape(cols // 8, 8, depth).sum(axis=0)

    def back(bx):
        return remote(
            phi.at[pl.ds(bx * rows, rows)], waves.at[pair * 2 * nl + me_g],
            bsend.at[bx], brecv.at[lax.rem(me_g, nl)], (bx * 2 + core, owner_v),
        )

    lane_row = lax.broadcasted_iota(jnp.int32, (nl, depth), 1)

    def products(buffer, slots):
        def one(j, acc):
            other = held[j]
            parts_of = [
                jnp.sum(jnp.sum(buffer[me_v * nl + s] * other, axis=0), axis=0, keepdims=True)
                for s in slots
            ]
            value = jnp.sum(jnp.concatenate(parts_of, axis=0), axis=1, keepdims=True)
            return jnp.where(lane_row[: len(slots)] == j, value, acc)

        return lax.fori_loop(0, nvec, one, jnp.zeros((len(slots), depth), jnp.float32), unroll=4)

    def spread(message, inbox, send, recv):
        inbox[me_g, me_v] = message[...]

        def start(k, carry):
            remote(message, inbox.at[me_g, me_v], send.at[k], recv.at[me], device_at(k)).start()
            return carry

        lax.fori_loop(1, total_devices, start, 0)

    def collect(message, inbox, send, recv, slot):
        def wait(k, carry):
            g, v = device_at(k)
            copy = remote(message, inbox.at[g, v], send.at[k], recv.at[g * parts + v], (g, v))
            copy.wait_recv()
            copy.wait_send()
            return carry

        lax.fori_loop(1, total_devices, wait, 0)
        for v in range(parts):
            total = inbox[0, v]
            for g in range(1, groups):
                total = total + inbox[g, v]
            mats[slot, v * nl : (v + 1) * nl] = total / (groups * rows * cols * depth)

    norm_now = alpha = None
    for step in range(ITERS):
        lax.fori_loop(0, length, pass_xz, 0, unroll=4)
        for side, bx in halos:
            halo(side, bx).wait_recv()
        zero = jnp.zeros((cols, depth), jnp.float32)
        norm, product = lax.fori_loop(0, length, pass_y, (zero, zero), unroll=4)
        sums[step, 0] = folded(norm)
        sums[step, 1] = folded(product)
        exchange = remote(sums.at[step], sums_in.at[step], ssend.at[step], srecv.at[step], partner)
        exchange.start()
        for side, bx in halos:
            halo(side, bx).wait_send()
        if step == 0:
            for q in range(1, pairs):
                trial_copy(q).wait_recv()
                trial_relay(q).start()
        if step == 1:
            trial_copy(0).wait_recv()
            for q in range(1, pairs):
                trial_relay(q).wait_recv()
            gmsg[...] = products(held, range(nl))
            spread(gmsg, gin, gsend, grecv)
        exchange.wait()
        norm_next = jnp.sum(sums[step, 0] + sums_in[step, 0], axis=(0, 1), keepdims=True)
        product = jnp.sum(sums[step, 1] + sums_in[step, 1], axis=(0, 1), keepdims=True)
        last = step + 1 == ITERS
        if step == 0:
            alpha = norm_next / product
            ratio = None
        else:
            ratio = norm_next / norm_now
            alpha = norm_next / (product - ratio * norm_next / alpha)
            ratio_wide = jnp.broadcast_to(ratio, (cols, depth))
        norm_now = norm_next
        alpha_wide = jnp.broadcast_to(alpha, (cols, depth))

        def update(x, carry):
            value = pad[x, center]
            image = img[x]
            if step == 0:
                phi[x] = alpha_wide * value
                dirn[x] = value
                along[x] = image
            else:
                value_dir = value + ratio_wide * dirn[x]
                phi[x] = phi[x] + alpha_wide * value_dir
                if not last:
                    dirn[x] = value_dir
                    image = image + ratio_wide * along[x]
                    along[x] = image
            if not last:
                pad[x, center] = value - alpha_wide * image
            return carry

        if not last:
            for bx in range(blocks):
                lax.fori_loop(bx * rows, (bx + 1) * rows, update, 0, unroll=rows)
                for side in range(2):
                    halo(side, bx).start()
        else:
            for bx in range(blocks):
                lax.fori_loop(
                    0, rows, lambda i, carry: update(bx * rows + i, carry), 0, unroll=rows
                )
                own = jnp.logical_and(bx * 2 + core == me_g, owner_v == me_v)

                @pl.when(jnp.logical_not(own))
                def _():
                    back(bx).start()

                @pl.when(own)
                def _():
                    waves[pair * 2 * nl + me_g] = phi[pl.ds(bx * rows, rows)]

    def wave_core(s):
        slot = waves.at[me_v * nl + s]
        return remote(slot, slot, psend.at[s], precv.at[s], partner)

    def wave_over(q, s):
        slot = waves.at[me_v * nl + s]
        return remote(
            slot, slot, xsend.at[q, s], xrecv.at[q, s], (me_g, lax.rem(pair + q, pairs) * 2 + core)
        )

    def wave_from(q, s):
        slot = waves.at[from_pair(q) * nl + s]
        return remote(slot, slot, xsend.at[q, s], xrecv.at[q, s], partner)

    def wave_relay(q, s):
        slot = waves.at[from_pair(q) * nl + s]
        return remote(slot, slot, ysend.at[q, s], yrecv.at[q, s], partner)

    collect(gmsg, gin, gsend, grecv, 0)
    gram = mats[0]
    row_of = lax.broadcasted_iota(jnp.int32, (nvec, depth), 0)
    lane_of = lax.broadcasted_iota(jnp.int32, (nvec, depth), 1)
    inverse = jnp.where(row_of == lane_of, 1.0, 0.0)
    for k in range(nvec):
        scale = 1.0 / jnp.sqrt(gram[k : k + 1, k : k + 1])
        column = gram[:, k : k + 1] * scale
        line = inverse[k : k + 1] * scale
        inverse = jnp.where(row_of > k, inverse - column * line, jnp.where(row_of == k, line, inverse))
        gram = gram - column * (gram[k : k + 1] * scale)
    mats[1] = inverse
    own_rows = mats[1, pl.ds(me_v * nl, nl)]
    for i in range(nvec):
        coef[i] = jnp.broadcast_to(own_rows[:, i : i + 1], (nl, depth))

    def rotate(buffer, out, base, count, fresh):
        def one(row, carry):
            totals = [None if fresh else out[s, row] for s in range(nl)]
            for i in range(count):
                value = buffer[base + i, row]
                for s in range(nl):
                    term = coef[base + i, s : s + 1] * value
                    totals[s] = term if totals[s] is None else totals[s] + term
            for s in range(nl):
                out[s, row] = totals[s]
            return carry

        lax.fori_loop(0, rows, one, 0)

    rotate(held, rotated, 0, nvec, True)
    for s in range(nl):
        @pl.when(jnp.logical_not(own_slot(s)))
        def _():
            slot = waves.at[me_v * nl + s]
            remote(phi.at[0:rows], slot, bsend.at[0], brecv.at[s], partner).wait_recv()

        for q in range(1, pairs):
            wave_over(q, s).start()
        wave_core(s).start()
        if 2 * (s + 1) == nl:
            cmsg[: nl // 2] = products(waves, range(nl // 2))

    cmsg[nl // 2 :] = products(waves, range(nl // 2, nl))
    spread(cmsg, cin, csend, crecv)
    for q in range(1, pairs):
        for s in range(nl):
            wave_from(q, s).wait_recv()
            wave_relay(q, s).start()

    for s in range(nl):
        slot = waves.at[(pair * 2 + 1 - core) * nl + s]
        remote(slot, slot, psend.at[s], precv.at[s], partner).wait_recv()
    rotate(waves, potentials, pair * 2 * nl, 2 * nl, True)
    for q in range(1, pairs):
        for s in range(nl):
            wave_relay(q, s).wait_recv()
        rotate(waves, potentials, lax.rem(pair - q + pairs, pairs) * 2 * nl, 2 * nl, False)

    collect(cmsg, cin, csend, crecv, 2)
    cross = mats[2]
    high = lax.Precision.HIGHEST
    last_dims = (((1,), (1,)), ((), ()))
    inverse = mats[1]
    small = inverse[:, :nvec]
    middle = 0.5 * (
        jnp.dot(small, cross, precision=high)[:, :nvec]
        + lax.dot_general(inverse, cross, last_dims, precision=high)
    )
    ritz[...] = lax.dot_general(middle, small, last_dims, precision=high)

    for s in range(nl):
        @pl.when(jnp.logical_not(own_slot(s)))
        def _():
            forward(s).wait_send()

        wave_core(s).wait_send()
    for bx in range(blocks):
        @pl.when(jnp.logical_not(jnp.logical_and(bx * 2 + core == me_g, owner_v == me_v)))
        def _():
            back(bx).wait_send()
    for q in range(pairs):
        trial_copy(q).wait_send()
    for q in range(1, pairs):
        trial_relay(q).wait_send()
        for s in range(nl):
            wave_over(q, s).wait_send()
            wave_relay(q, s).wait_send()


def paired_body(trial_block, response_weight):
    nl, rows, cols, depth = trial_block.shape
    groups, parts = lax.axis_size("grid"), lax.axis_size("vec")
    nvec, blocks = parts * nl, groups // 2
    pairs, length, devices = parts // 2, (groups // 2) * rows, groups * parts
    f32 = jnp.float32
    dma = pltpu.SemaphoreType.DMA
    vmem = pl.BlockSpec(memory_space=pltpu.VMEM)
    field = pltpu.VMEM((length, cols, depth), f32)
    whole = pltpu.VMEM((nvec, rows, cols, depth), f32)
    inbox = pltpu.VMEM((groups, parts, nl, depth), f32)
    message = pltpu.VMEM((nl, depth), f32)
    small = pltpu.VMEM((ITERS, 2, 8, depth), f32)
    return pl.pallas_call(
        functools.partial(kernel, groups, parts),
        out_shape=(
            pltpu.VMEM(trial_block.shape, f32),
            pltpu.VMEM(trial_block.shape, f32),
            pltpu.VMEM((nvec, nvec), f32),
        ),
        in_specs=[pl.BlockSpec(memory_space=pl.ANY)] * 2,
        out_specs=(vmem, vmem, vmem),
        scratch_shapes=[
            pltpu.VMEM((rows, cols, depth), f32),
            pltpu.VMEM((nl, rows, cols, depth), f32),
            pltpu.VMEM((length, cols + 2 * PAD, depth), f32),
            field, field, field, field, small, small, whole, whole,
            message, inbox, message, inbox,
            pltpu.VMEM((3, nvec, depth), f32), pltpu.VMEM((nvec, nl, depth), f32),
            dma((nl,)), dma((blocks,)), dma((2, blocks)), dma((2, blocks)),
            dma((ITERS,)), dma((ITERS,)), dma((pairs,)), dma((pairs,)), dma((pairs,)), dma((pairs,)),
            dma((blocks,)), dma((nl,)), dma((nl,)), dma((nl,)),
            dma((pairs, nl)), dma((pairs, nl)), dma((pairs, nl)), dma((pairs, nl)),
            dma((devices,)), dma((devices,)), dma((devices,)), dma((devices,)), dma((2,)),
        ],
        compiler_params=pltpu.CompilerParams(collective_id=0, has_side_effects=True),
    )(trial_block, response_weight)


def chosen_body(trial_block, response_weight):
    nl, rows, cols, depth = trial_block.shape
    groups, parts = lax.axis_size("grid"), lax.axis_size("vec")
    fits = (
        max(groups // 16, 2) == 2 and groups == 2 * nl and parts % 2 == 0 and rows == HALO
        and cols % 8 == 0 and cols >= PAD and parts * nl <= depth
    )
    return (paired_body if fits else body)(trial_block, response_weight)


def solution(mesh):
    placed = (P("vec", "grid", None, None), P("grid", None, None))
    return jax.shard_map(
        chosen_body,
        mesh=mesh,
        in_specs=placed,
        out_specs=(P("vec", "grid", None, None), P("vec", "grid", None, None), P()),
        check_vma=False,
    )
```
